32 devices in a mesh: dp: 8 (over z, core), tensor: 4 (over y, x).
Axes of the slice: x: 2, y: 2, z: 4, core: 2. Of those that a mesh axis runs over, the one named last changes fastest.
Arguments:
- tokens: bfloat16 [8192, 2048], P(('dp', 'tensor')), may hold values from -6 to 6
- lengths: int32 [8], P('dp'), may hold values from 512 to 1024, as said below
- routes: int32 [8192, 4], P(('dp', 'tensor')), may hold values from 0 to 7, all different within a row; in each aligned block of 256 rows (0 to 255, 256 to 511, ...) at most 192 rows name the same one
- attn_gain: float32 [2048], replicated, may hold values from 0.5 to 1.5
- w_query: bfloat16 [2048, 2048], P('dp', 'tensor')
- w_key: bfloat16 [2048, 2048], P('dp', 'tensor'), may hold values from -0.125 to 0.125
- w_value: bfloat16 [2048, 2048], P('dp', 'tensor'), may hold values from -0.125 to 0.125
- w_output: bfloat16 [2048, 2048], P('tensor', 'dp'), may hold values from -0.5 to 0.5
- moe_gain: float32 [2048], replicated, may hold values from 0.5 to 1.5
- w_router: float32 [2048, 8], replicated, may hold values from -0.0625 to 0.0625
- w_sigmoid: float32 [2048], replicated, may hold values from -0.125 to 0.125
- shared_gate: bfloat16 [2048, 5632], P('dp', 'tensor'), may hold values from -0.125 to 0.125
- shared_up: bfloat16 [2048, 5632], P('dp', 'tensor'), may hold values from -0.125 to 0.125
- shared_down: bfloat16 [5632, 2048], P('tensor', 'dp'), may hold values from -0.15625 to 0.15625
- expert_gate: bfloat16 [8, 2048, 1408], P('dp', 'tensor'), may hold values from -0.125 to 0.125
- expert_up: bfloat16 [8, 2048, 1408], P('dp', 'tensor'), may hold values from -0.125 to 0.125
- expert_down: bfloat16 [8, 1408, 2048], P('dp', None, 'tensor'), may hold values from -0.3125 to 0.3125
- cotangent: bfloat16 [8192, 2048], P(('dp', 'tensor')), may hold values from -6 to 6
Outputs:
- block_out: bfloat16 [8192, 2048], P(('dp', 'tensor'))
- d_tokens: float32 [8192, 2048], P(('dp', 'tensor'))
- d_attn_gain: float32 [2048], replicated
- d_w_query: float32 [2048, 2048], P('dp', 'tensor')
- d_w_key: float32 [2048, 2048], P('dp', 'tensor')
- d_w_value: float32 [2048, 2048], P('dp', 'tensor')
- d_w_output: float32 [2048, 2048], P('tensor', 'dp')
- d_moe_gain: float32 [2048], replicated
- d_w_router: float32 [2048, 8], replicated
- d_w_sigmoid: float32 [2048], replicated
- d_shared_gate: float32 [2048, 5632], P('dp', 'tensor')
- d_shared_up: float32 [2048, 5632], P('dp', 'tensor')
- d_shared_down: float32 [5632, 2048], P('tensor', 'dp')
- d_expert_gate: float32 [8, 2048, 1408], P('dp', 'tensor')
- d_expert_up: float32 [8, 2048, 1408], P('dp', 'tensor')
- d_expert_down: float32 [8, 1408, 2048], P('dp', None, 'tensor')
- clip_scale: float32 [16], P('tensor')
- query_clipped: bfloat16 [2048, 2048], P('dp', 'tensor')
- key_clipped: bfloat16 [2048, 2048], P('dp', 'tensor')
The draws below stay inside these ranges and needn't reach their ends.
Inputs may be any that keep to these rules, and one draw needn't show every extreme that they name: Positions from lengths[s] to 1023 of sequence s are padding; the first sequence has none. Among the rows of one device no expert is named by more than 192 routes.
All inputs are finite; a program needn't handle non-finite values.
Results may differ from the reference program's by a relative error of at most 0.024.
Values may be sent and summed in bfloat16 or wider, within the bound.
No kernel may reach another device: no remote copies, remote signals or barrier semaphores. Data moves between devices by JAX's collectives and lax.ppermute only.
A program may use at most 320 MiB of HBM per device.

```python
import math
import jax
import jax.numpy as jnp
import numpy as np
from jax import lax

D = 2048
H = 16
DH = 128
FE = 1408
FS = 5632
TOP = 4
LEN = 1024
ROWS = 256
SEQS = 8
TOKENS = 8192
EXPERTS = 8
CAP = 192
N_DP = 8
N_TENSOR = 4


def draw_lengths(key, part):
    drawn = jax.random.randint(key, (SEQS,), LEN // 2, LEN + 1, dtype=jnp.int32)
    return drawn.at[0].set(LEN)


def draw_w_query(key, part):
    spread = jnp.exp(jax.random.uniform(jax.random.fold_in(key, 7), (H,), jnp.float32, 0.0, 1.0986123))
    columns = jnp.repeat(spread, DH)
    base = jax.random.normal(key, (D, H * DH), jnp.float32)
    return (base * D ** (-0.5) * columns[None, :]).astype(jnp.bfloat16)


def level_of(stream_key, dims, pieces, smallest, high):
    factor_of, own = 1.0, jax.random.fold_in(stream_key, 6)
    for axis_at, blocks in pieces:
        heights = jnp.exp(jax.random.uniform(jax.random.fold_in(own, axis_at), (blocks,), jnp.float32, smallest / len(pieces), high / len(pieces)))
        factor_of = factor_of * jnp.repeat(heights, dims[axis_at] // blocks).reshape([-1 if axis == axis_at else 1 for axis in range(len(dims))])
    return factor_of


def deal_out(own_key, own, number, rows, amount, top, bound, slope):
    order = jax.random.permutation(own_key, amount)
    heavy_load, common = portions_of(amount, rows * top, bound, slope, True), portions_of(amount, rows * top, bound, slope, False)
    places = jnp.arange(amount)

    def named(sizes, turn):
        used = int((sizes > 0).sum())
        fixed = max(1, used // 4)
        shifted = fixed + (places - fixed + turn * (used - fixed)) % max(1, amount - fixed)
        return jnp.zeros((amount,), jnp.int32).at[order[jnp.where(places < fixed, places, shifted)]].set(jnp.asarray(sizes, jnp.int32))

    sizes = jnp.where(number % 4 == 0, named(heavy_load, number // 4), named(common, number - number // 4 - 1))
    mixed = jax.random.permutation(jax.random.fold_in(own, 3), amount)
    giver, sink = mixed[0:amount // 2 * 2:2], mixed[1:amount // 2 * 2:2]
    margin = jnp.minimum(sizes[giver] - 1, bound - sizes[sink]) // 2
    margin = jnp.where((giver == order[0]) | (sink == order[0]) | (sizes[sink] == 0), 0, jnp.maximum(margin, 0))
    shifted = jax.random.randint(jax.random.fold_in(own, 4), (amount // 2,), 0, 1 << 20) % (margin + 1)
    sizes = sizes.at[giver].add(-shifted).at[sink].add(shifted)
    members = jnp.searchsorted(jnp.cumsum(sizes), jnp.arange(rows * top), side="right").astype(jnp.int32)
    listing = members.reshape(top, rows).T
    listing = listing[jax.random.permutation(jax.random.fold_in(own, 1), rows)]
    turn = jax.random.randint(jax.random.fold_in(own, 2), (rows, 1), 0, top)
    return jnp.take_along_axis(listing, (jnp.arange(top)[None, :] + turn) % top, axis=1)


def portions_of(amount, total, limit, slope, full):
    weights = [(1 << 20) // math.isqrt(rank ** slope) + 1 for rank in range(1, amount + 1)]
    largest = limit if full else min(limit, max(-(-total // amount), total * weights[0] // sum(weights)))
    least = 1 if total - largest >= amount - 1 else 0
    given, spare = [largest] + [least] * (amount - 1), total - largest - least * (amount - 1)
    while spare > 0:
        free = [i for i in range(1, amount) if given[i] < largest] or [i for i in range(1, amount) if given[i] < limit]
        mass, budget = sum([weights[i] for i in free]), spare
        for i in free:
            more = min(limit - given[i], max(1, budget * weights[i] // mass), spare)
            given[i] = given[i] + more
            spare = spare - more
    return np.array(given)


def scatter_about(rng, extent, scale, bound, pieces=(), kind=jnp.bfloat16):
    loudness = level_of(rng, extent, pieces, -0.22, 0.18) if pieces else 1.0
    result = jax.random.normal(rng, extent, jnp.float32) * scale * loudness
    return jnp.minimum(jnp.maximum(result, -bound), bound).astype(kind)


def setup_inputs(seed: int = 0) -> dict:
    key_of = jax.random.split(jax.random.key(seed), 19)
    tokens = scatter_about(key_of[0], (TOKENS, D), 1.0, 6.0, ((0, 32),))
    lengths = draw_lengths(jax.random.fold_in(key_of[18], 71), 0)
    routes_keys = jax.random.split(jax.random.fold_in(key_of[2], 1), TOKENS // ROWS)
    routes_turns = jax.random.permutation(jax.random.fold_in(key_of[2], 3), TOKENS // ROWS)
    routes = jax.vmap(lambda own, number: deal_out(jax.random.fold_in(key_of[2], 2), own, number, ROWS, EXPERTS, TOP, CAP, 2))(routes_keys, routes_turns).reshape((TOKENS, TOP))
    attn_gain = jnp.clip(1.0 + 0.1 * jax.random.normal(key_of[3], (D,), jnp.float32), 0.5, 1.5)
    w_query = draw_w_query(jax.random.fold_in(key_of[18], 71), 0)
    w_key = scatter_about(key_of[5], (D, H * DH), D ** -0.5, 0.125, ((0, 8), (1, 4)))
    w_value = scatter_about(key_of[6], (D, H * DH), D ** -0.5, 0.125, ((0, 8), (1, 4)))
    w_output = scatter_about(key_of[7], (H * DH, D), (H * DH // 16) ** -0.5, 0.5, ((0, 4), (1, 8)))
    moe_gain = jnp.clip(1.0 + 0.1 * jax.random.normal(key_of[8], (D,), jnp.float32), 0.5, 1.5)
    w_router = scatter_about(key_of[9], (D, EXPERTS), (4 * D) ** -0.5, 0.0625, (), jnp.float32)
    w_sigmoid = scatter_about(key_of[10], (D,), D ** -0.5, 0.125, (), jnp.float32)
    shared_gate = scatter_about(key_of[11], (D, FS), D ** -0.5, 0.125, ((0, 8), (1, 4)))
    shared_up = scatter_about(key_of[12], (D, FS), D ** -0.5, 0.125, ((0, 8), (1, 4)))
    shared_down = scatter_about(key_of[13], (FS, D), (FS // 4) ** -0.5, 0.15625, ((0, 4), (1, 8)))
    expert_gate = scatter_about(key_of[14], (EXPERTS, D, FE), D ** -0.5, 0.125, ((0, 8), (1, 4)))
    expert_up = scatter_about(key_of[15], (EXPERTS, D, FE), D ** -0.5, 0.125, ((0, 8), (1, 4)))
    expert_down = scatter_about(key_of[16], (EXPERTS, FE, D), (FE // 4) ** -0.5, 0.3125, ((0, 8), (2, 4)))
    cotangent = scatter_about(key_of[17], (TOKENS, D), 1.0, 6.0, ((0, 32),))
    return dict(tokens=tokens, lengths=lengths, routes=routes, attn_gain=attn_gain, w_query=w_query, w_key=w_key, w_value=w_value, w_output=w_output, moe_gain=moe_gain, w_router=w_router, w_sigmoid=w_sigmoid, shared_gate=shared_gate, shared_up=shared_up, shared_down=shared_down, expert_gate=expert_gate, expert_up=expert_up, expert_down=expert_down, cotangent=cotangent)


EPS = 1e-06
CLIP_LIMIT = 6.0
NEG = -1e+30
HIGH = lax.Precision.HIGHEST

@jax.custom_vjp
def low(v):
    return lax.optimization_barrier(v.astype(jnp.bfloat16)).astype(jnp.float32)

@jax.custom_vjp
def low_back(v):
    return v

def low_keep(v):
    return (low(v), None)

def low_pass(kept, grad):
    return (grad,)

def back_keep(v):
    return (v, None)

def back_low(kept, grad):
    return (low(grad),)
low.defvjp(low_keep, low_pass)
low_back.defvjp(back_keep, back_low)

def matmul(left, right):
    return jnp.dot(left, right, precision=HIGH)

def rms_norm(inputs, gain):
    return inputs * lax.rsqrt(lax.optimization_barrier(jnp.mean(inputs * inputs, axis=-1, keepdims=True)) + EPS) * gain

def slot_table(routes):
    devices = N_DP * N_TENSOR
    blocks = routes.reshape(devices, ROWS * TOP)
    onehot = (blocks[:, :, None] == jnp.arange(EXPERTS, dtype=jnp.int32)[None, None, :]).astype(jnp.int32)
    earlier = jnp.cumsum(onehot, axis=1) - onehot
    placed = lax.optimization_barrier(jnp.sum(earlier * onehot, axis=2))
    device_ids = jnp.arange(devices, dtype=jnp.int32)[:, None]
    flat_slot = (blocks * (devices * CAP) + device_ids * CAP + placed).reshape(-1).astype(jnp.int32)
    pair_ids = jnp.arange(TOKENS * TOP, dtype=jnp.int32)
    slot_owner = jnp.full((EXPERTS * devices * CAP,), TOKENS * TOP, jnp.int32).at[flat_slot].set(pair_ids)
    return (flat_slot, slot_owner)

def attend(packed):
    queries, keys_in, values_in, length = packed
    position = jnp.arange(LEN, dtype=jnp.int32)
    allowed = (position[None, :] <= position[:, None]) & (position[None, :] < length)
    raw_scores = jnp.einsum('qhd,khd->hqk', queries, keys_in, precision=HIGH) * DH ** (-0.5)
    scores = low_back(jnp.where(allowed[None], raw_scores, NEG))
    weights = low(jax.nn.softmax(scores, axis=-1))
    attended = low(low_back(jnp.einsum('hqk,khd->qhd', weights, values_in, precision=HIGH)))
    counted = allowed & (position[:, None] < length)
    highest = lax.optimization_barrier(jnp.max(jnp.where(counted[None], raw_scores, NEG), axis=(1, 2)))
    return (attended.reshape(LEN, H * DH), highest)

def expert_apply(packed):
    inputs, gate_weight, up_weight, down_weight = packed
    gate_pre = low_back(matmul(inputs, gate_weight))
    up_pre = low_back(matmul(inputs, up_weight))
    hidden = low(jax.nn.silu(gate_pre) * up_pre)
    return low(low_back(matmul(hidden, down_weight)))

def layer(tokens_in, params, lengths, routes, flat_slot, slot_owner):
    attn_gain, w_query, w_key, w_value, w_output, moe_gain, w_router, w_sigmoid, shared_gate, shared_up, shared_down, expert_gate, expert_up, expert_down = params
    normed = low(rms_norm(tokens_in, attn_gain))
    queries = low(low_back(matmul(normed, w_query)))
    keys_all = low(low_back(matmul(normed, w_key)))
    values_all = low(low_back(matmul(normed, w_value)))
    seq_shape = (SEQS, LEN, H, DH)
    attended, highest = lax.map(jax.checkpoint(attend), (queries.reshape(seq_shape), keys_all.reshape(seq_shape), values_all.reshape(seq_shape), lengths))
    attended = attended.reshape(TOKENS, H * DH)
    middle = tokens_in + low_back(matmul(attended, w_output))
    moe_in = low(rms_norm(middle, moe_gain))
    logits = matmul(moe_in, w_router)
    picked = routes[:, :, None] == jnp.arange(EXPERTS, dtype=jnp.int32)[None, None, :]
    chosen = lax.optimization_barrier(jnp.sum(jnp.where(picked, logits[:, None, :], 0.0), axis=2))
    gates = jax.nn.softmax(chosen, axis=1)
    padded = jnp.concatenate([moe_in, jnp.zeros((1, D), jnp.float32)], axis=0)
    dispatched = low_back(padded[slot_owner // TOP]).reshape(EXPERTS, -1, D)
    expert_out = lax.map(jax.checkpoint(expert_apply), (dispatched, expert_gate, expert_up, expert_down))
    pair_out = expert_out.reshape(-1, D)[flat_slot].reshape(TOKENS, TOP, D)
    routed = lax.optimization_barrier(jnp.sum(gates[:, :, None] * pair_out, axis=1))
    gate_pre = low_back(matmul(moe_in, shared_gate))
    up_pre = low_back(matmul(moe_in, shared_up))
    shared_hidden = low(jax.nn.silu(gate_pre) * up_pre)
    shared_out = low_back(matmul(shared_hidden, shared_down))
    mixing = jax.nn.sigmoid(matmul(moe_in, w_sigmoid))
    return (middle + routed + mixing[:, None] * shared_out, lax.optimization_barrier(jnp.max(highest, axis=0)))

def reference(tokens, lengths, routes, attn_gain, w_query, w_key, w_value, w_output, moe_gain, w_router, w_sigmoid, shared_gate, shared_up, shared_down, expert_gate, expert_up, expert_down, cotangent):
    params = tuple((member.astype(jnp.float32) for member in (attn_gain, w_query, w_key, w_value, w_output, moe_gain, w_router, w_sigmoid, shared_gate, shared_up, shared_down, expert_gate, expert_up, expert_down)))
    flat_slot, slot_owner = slot_table(routes)

    def forward(tokens_in, weights_in):
        return layer(tokens_in, weights_in, lengths, routes, flat_slot, slot_owner)
    block_out, pull_back, highest = jax.vjp(forward, tokens.astype(jnp.float32), params, has_aux=True)
    d_tokens, grads = pull_back(cotangent.astype(jnp.float32))
    clip_scale = jnp.sqrt(CLIP_LIMIT / jnp.maximum(highest, CLIP_LIMIT))
    columns = jnp.repeat(clip_scale, DH)
    query_clipped = (params[1] * columns[None, :]).astype(jnp.bfloat16)
    key_clipped = (params[2] * columns[None, :]).astype(jnp.bfloat16)
    return (block_out.astype(jnp.bfloat16), d_tokens, grads[0], grads[1], grads[2], grads[3], grads[4], grads[5], grads[6], grads[7], grads[8], grads[9], grads[10], grads[11], grads[12], grads[13], clip_scale, query_clipped, key_clipped)
```

```python
import jax
import jax.numpy as jnp
from jax import lax
from jax.sharding import PartitionSpec as P

DH = 128


EPS = 1e-06
CLIP_LIMIT = 6.0
NEG = -1e30
HIGH = lax.Precision.HIGHEST
CONTRACT_LAST = (((1,), (1,)), ((), ()))
CONTRACT_FIRST = (((0,), (0,)), ((), ()))


def norm_rows(inputs, gain):
    factor = lax.rsqrt(jnp.mean(inputs * inputs, axis=-1, keepdims=True) + EPS)
    return (inputs * factor * gain, factor)


def norm_back(inputs, factor, gain, upstream):
    scaled = upstream * gain
    inner = jnp.mean(scaled * inputs, axis=-1, keepdims=True)
    return (
        factor * scaled - inputs * (factor * factor * factor) * inner,
        jnp.sum(upstream * inputs * factor, axis=0),
    )


def pairs(count, bit):
    return [(index, index ^ bit) for index in range(count)]


def swap(values_in, bit, axis_name="tensor"):
    return lax.ppermute(values_in, axis_name, pairs(lax.axis_size(axis_name), bit))


def halves(values_in, axis):
    middle_at = values_in.shape[axis] // 2
    return (
        lax.slice_in_dim(values_in, 0, middle_at, axis=axis),
        lax.slice_in_dim(values_in, middle_at, values_in.shape[axis], axis=axis),
    )


def relay_gather(block):
    across = swap(block, 1)
    along = swap(block, 2)
    cut = 1 if block.ndim > 2 else 0
    first, _ = halves(along, cut)
    _, second = halves(across, cut)
    diagonal = jnp.concatenate([swap(first, 1), swap(second, 2)], axis=cut)
    here = lax.axis_index("tensor")
    odd, high = (here & 1) == 1, (here & 2) == 2
    low_even, low_odd = jnp.where(odd, across, block), jnp.where(odd, block, across)
    high_even, high_odd = jnp.where(odd, diagonal, along), jnp.where(odd, along, diagonal)
    return (
        jnp.where(high, high_even, low_even),
        jnp.where(high, high_odd, low_odd),
        jnp.where(high, low_even, high_even),
        jnp.where(high, low_odd, high_odd),
    )


def group_gather(block, axis):
    if lax.axis_size("tensor") != 4:
        return lax.all_gather(block, "tensor", axis=axis, tiled=True)
    return jnp.concatenate(relay_gather(block), axis=axis)


def group_scatter(partial, axis):
    count = lax.axis_size("tensor")
    if count != 4:
        return lax.psum_scatter(
            partial, "tensor", scatter_dimension=axis, tiled=True
        ).astype(jnp.float32)
    here = lax.axis_index("tensor")
    size = partial.shape[axis] // count

    def block(other):
        return lax.dynamic_slice_in_dim(partial, (here ^ other) * size, size, axis)

    cut = 1 if partial.ndim > 2 else 0
    far = halves(block(3), cut)
    over_x, over_y = swap(far[0], 1), swap(far[1], 2)
    near_y, near_x = halves(block(2), cut), halves(block(1), cut)
    wide = jnp.float32
    send_y = jnp.concatenate(
        [(near_y[0].astype(wide) + over_x.astype(wide)).astype(partial.dtype), near_y[1]], axis=cut
    )
    send_x = jnp.concatenate(
        [near_x[0], (near_x[1].astype(wide) + over_y.astype(wide)).astype(partial.dtype)], axis=cut
    )
    from_y, from_x = swap(send_y, 2), swap(send_x, 1)
    return block(0).astype(wide) + from_y.astype(wide) + from_x.astype(wide)


def column_gather(rows):
    return lax.all_gather(rows, "dp", axis=0, tiled=True)


def column_scatter(partial, axis):
    return lax.psum_scatter(
        partial.astype(jnp.bfloat16), "dp", scatter_dimension=axis, tiled=True
    ).astype(jnp.float32)


def trade(blocks, axis_name):
    return lax.all_to_all(blocks, axis_name, split_axis=0, concat_axis=0, tiled=True)


def butterfly(values_in, combine, axis_names):
    for axis_name in axis_names:
        bit = 1
        while bit < lax.axis_size(axis_name):
            values_in = combine(values_in, swap(values_in, bit, axis_name))
            bit *= 2
    return values_in


def times(left, right):
    return jnp.dot(left, right, preferred_element_type=jnp.float32)


def times_last(left, right):
    return lax.dot_general(left, right, CONTRACT_LAST, preferred_element_type=jnp.float32)


def times_first(left, right):
    return lax.dot_general(left, right, CONTRACT_FIRST, preferred_element_type=jnp.float32)


def slice_width(hidden_width, share):
    return -(-hidden_width // (128 * share)) * 128


def spread_in(weights):
    count, owners = lax.axis_size("tensor"), lax.axis_size("dp")
    share = owners // count
    rows, hidden_width = weights[0].shape
    width = slice_width(hidden_width, share)
    piece = rows // count
    padded = jnp.stack(
        [jnp.pad(w, ((0, 0), (0, share * width - hidden_width))) for w in weights], axis=0
    )
    blocks = padded.reshape(2, count, piece, share * width).transpose(1, 0, 2, 3)
    blocks = trade(blocks, "tensor").reshape(count, 2, piece, share, width)
    blocks = blocks.transpose(0, 3, 1, 2, 4).reshape(owners, 2, piece, width)
    blocks = trade(blocks, "dp")
    whole = group_gather(blocks.reshape(1, owners, 2, piece, width), 0)
    whole = whole.transpose(2, 1, 0, 3, 4).reshape(2, owners * rows, width)
    return whole[0], whole[1]


def spread_in_back(grads, rows, hidden_width):
    count, owners = lax.axis_size("tensor"), lax.axis_size("dp")
    share = owners // count
    width = grads[0].shape[1]
    piece = rows // count
    stacked = jnp.stack(grads, axis=0).reshape(2, owners, count, piece, width)
    stacked = stacked.transpose(2, 1, 0, 3, 4)
    blocks = group_scatter(stacked, 0).astype(jnp.bfloat16).reshape(owners, 2, piece, width)
    blocks = trade(blocks, "dp").reshape(count, share, 2, piece, width)
    blocks = blocks.transpose(0, 2, 3, 1, 4).reshape(count, 2, piece, share * width)
    blocks = trade(blocks, "tensor").transpose(1, 0, 2, 3).reshape(2, rows, share * width)
    blocks = blocks[:, :, :hidden_width].astype(jnp.float32)
    return blocks[0], blocks[1]


def spread_out(weight):
    count, owners = lax.axis_size("tensor"), lax.axis_size("dp")
    share = owners // count
    hidden_width, columns = weight.shape
    width = slice_width(hidden_width, share)
    padded = jnp.pad(weight, ((0, share * width - hidden_width), (0, 0)))
    blocks = padded.reshape(share, count, width // count, columns).transpose(1, 0, 2, 3)
    blocks = trade(blocks, "tensor").reshape(owners, width // count, columns)
    blocks = trade(blocks, "dp").transpose(1, 0, 2).reshape(width // count, owners * columns)
    return group_gather(blocks, 0)


def spread_out_back(grad, hidden_width, columns):
    count, owners = lax.axis_size("tensor"), lax.axis_size("dp")
    share = owners // count
    width = grad.shape[0]
    piece = width // count
    blocks = group_scatter(grad, 0).astype(jnp.bfloat16).reshape(piece, owners, columns)
    blocks = trade(blocks.transpose(1, 0, 2), "dp").reshape(count, share, piece, columns)
    blocks = trade(blocks, "tensor").transpose(1, 0, 2, 3).reshape(share * width, columns)
    return blocks[:hidden_width].astype(jnp.float32)


def attention_forward(queries, keys_in, values_in, length, factor):
    seq_len = queries.shape[0]
    block_len = min(512, seq_len)
    position = jnp.arange(seq_len, dtype=jnp.int32)

    def one_block(offset):
        rows_here = offset + jnp.arange(block_len, dtype=jnp.int32)
        query_block = lax.dynamic_slice_in_dim(queries, offset, block_len, 0)
        allowed = (position[None, :] <= rows_here[:, None]) & (position[None, :] < length)
        raw_scores = (
            jnp.einsum("qhd,khd->hqk", query_block, keys_in, preferred_element_type=jnp.float32)
            * factor
        )
        scores = jnp.where(allowed[None], raw_scores, NEG)
        highest = jnp.max(scores, axis=2, keepdims=True)
        log_total = highest + jnp.log(jnp.sum(jnp.exp(scores - highest), axis=2, keepdims=True))
        weights = jnp.exp(scores - log_total).astype(jnp.bfloat16)
        attended = jnp.einsum(
            "hqk,khd->qhd", weights, values_in, preferred_element_type=jnp.float32
        )
        counted = allowed & (rows_here[:, None] < length)
        peak_here = jnp.max(jnp.where(counted[None], raw_scores, NEG), axis=(1, 2))
        return (attended.astype(jnp.bfloat16), log_total[:, :, 0], peak_here)

    offsets = jnp.arange(seq_len // block_len, dtype=jnp.int32) * block_len
    attended, log_totals, peaks = lax.map(one_block, offsets)
    return (attended.reshape(seq_len, -1), log_totals, jnp.max(peaks, axis=0))


def attention_backward(queries, keys_in, values_in, grad_out, log_totals, length, factor):
    seq_len = queries.shape[0]
    block_len = log_totals.shape[2]
    position = jnp.arange(seq_len, dtype=jnp.int32)

    def one_block(sums, packed):
        key_sum, value_sum = sums
        offset, log_total = packed
        rows_here = offset + jnp.arange(block_len, dtype=jnp.int32)
        query_block = lax.dynamic_slice_in_dim(queries, offset, block_len, 0)
        grad_block = lax.dynamic_slice_in_dim(grad_out, offset, block_len, 0)
        allowed = (position[None, :] <= rows_here[:, None]) & (position[None, :] < length)
        raw_scores = (
            jnp.einsum("qhd,khd->hqk", query_block, keys_in, preferred_element_type=jnp.float32)
            * factor
        )
        scores = jnp.where(allowed[None], raw_scores, NEG)
        probs = jnp.exp(scores - log_total[:, :, None])
        weights = probs.astype(jnp.bfloat16)
        along = jnp.einsum(
            "qhd,khd->hqk", grad_block, values_in, preferred_element_type=jnp.float32
        )
        inner = jnp.sum(probs * along, axis=2, keepdims=True)
        grad_scores = (probs * (along - inner)).astype(jnp.bfloat16)
        grad_query = (
            jnp.einsum("hqk,khd->qhd", grad_scores, keys_in, preferred_element_type=jnp.float32)
            * factor
        )
        key_sum = (
            key_sum
            + jnp.einsum(
                "hqk,qhd->khd", grad_scores, query_block, preferred_element_type=jnp.float32
            )
            * factor
        )
        value_sum = value_sum + jnp.einsum(
            "hqk,qhd->khd", weights, grad_block, preferred_element_type=jnp.float32
        )
        return ((key_sum, value_sum), grad_query.astype(jnp.bfloat16))

    offsets = jnp.arange(seq_len // block_len, dtype=jnp.int32) * block_len
    start_zero = jnp.zeros(keys_in.shape, jnp.float32)
    (key_sum, value_sum), grad_query = lax.scan(
        one_block, (start_zero, start_zero), (offsets, log_totals)
    )
    return (
        grad_query.reshape(seq_len, -1),
        key_sum.astype(jnp.bfloat16).reshape(seq_len, -1),
        value_sum.astype(jnp.bfloat16).reshape(seq_len, -1),
    )


def local(
    tokens,
    lengths,
    routes,
    attn_gain,
    w_query,
    w_key,
    w_value,
    w_output,
    moe_gain,
    w_router,
    w_sigmoid,
    shared_gate,
    shared_up,
    shared_down,
    expert_gate,
    expert_up,
    expert_down,
    cotangent,
):
    low = jnp.bfloat16
    factor = DH ** (-0.5)
    inputs = tokens.astype(jnp.float32)
    normed, inv_one = norm_rows(inputs, attn_gain)
    gathered_one = group_gather(normed.astype(low), 0)
    seq_len = gathered_one.shape[0]
    width = w_query.shape[1]
    in_weights = column_gather(jnp.concatenate([w_query, w_key, w_value], axis=1))
    out_weight = lax.all_gather(w_output, "dp", axis=1, tiled=True)
    projected = times(gathered_one, in_weights).astype(low)
    queries = projected[:, :width].reshape(seq_len, -1, DH)
    keys_in = projected[:, width : 2 * width].reshape(seq_len, -1, DH)
    values_in = projected[:, 2 * width :].reshape(seq_len, -1, DH)
    length = lengths[0]
    attended, log_totals, peaks = attention_forward(queries, keys_in, values_in, length, factor)
    peaks = butterfly(peaks, jnp.maximum, ("dp",))
    middle = inputs + group_scatter(times(attended, out_weight).astype(low), 0)
    moe_norm, inv_two = norm_rows(middle, moe_gain)
    moe_low = moe_norm.astype(low)
    moe_wide = moe_low.astype(jnp.float32)
    experts = w_router.shape[1]
    owners = lax.axis_size("dp")
    rows_dev, route_count = routes.shape
    column_rows = owners * rows_dev
    logits = jnp.dot(moe_wide, w_router, precision=HIGH)
    picked = (routes[:, :, None] == jnp.arange(experts, dtype=jnp.int32)[None, None, :]).astype(
        jnp.float32
    )
    chosen = jnp.sum(picked * logits[:, None, :], axis=2)
    gates = jax.nn.softmax(chosen, axis=1)
    mixing = jax.nn.sigmoid(jnp.dot(moe_wide, w_sigmoid, precision=HIGH))
    gate_of = jnp.sum(picked * gates[:, :, None], axis=1)
    scales = jnp.stack([gate_of.T, jnp.broadcast_to(mixing[None], (experts, rows_dev))], axis=1)
    scales = trade(scales, "dp")
    scale_routed = scales[:, 0].reshape(column_rows, 1)
    scale_shared = scales[:, 1].reshape(column_rows, 1)
    column = column_gather(moe_low)
    upstream_column = column_gather(cotangent)
    full_gate = group_gather(expert_gate[0], 0)
    full_up = group_gather(expert_up[0], 0)
    full_down = group_gather(expert_down[0], 1)
    part_gate, part_up = spread_in((shared_gate, shared_up))
    part_down = spread_out(shared_down)

    def branch(gate_weight, up_weight, down_weight, scale):
        gate_pre = times(column, gate_weight)
        up_pre = times(column, up_weight)
        raw = times_last(upstream_column, down_weight)
        sigma = jax.nn.sigmoid(gate_pre)
        activated = gate_pre * sigma
        hidden = activated * up_pre
        inner = jnp.sum(hidden * raw, axis=1)
        scaled = raw * scale
        d_gate = (scaled * up_pre * (sigma * (1.0 + gate_pre * (1.0 - sigma)))).astype(low)
        d_up = (scaled * activated).astype(low)
        hidden = (hidden * scale).astype(low)
        d_rows = times_last(d_gate, gate_weight) + times_last(d_up, up_weight)
        return (hidden, inner, d_gate, d_up, d_rows)

    hidden_e, inner_e, d_gate_e, d_up_e, d_rows_e = branch(
        full_gate, full_up, full_down, scale_routed
    )
    hidden_s, inner_s, d_gate_s, d_up_s, d_rows_s = branch(
        part_gate, part_up, part_down, scale_shared
    )
    d_moe = column_scatter((d_rows_e + d_rows_s).astype(low), 0)
    inner = trade(
        jnp.stack([inner_e.reshape(owners, rows_dev), inner_s.reshape(owners, rows_dev)], axis=1),
        "dp",
    )
    combined = middle + column_scatter(
        (times(hidden_e, full_down) + times(hidden_s, part_down)).astype(low), 0
    )
    upstream = cotangent.astype(jnp.float32)
    d_mixing = mixing * (1.0 - mixing) * jnp.sum(inner[:, 1], axis=0)
    d_gates = jnp.sum(picked * inner[:, 0].T[:, None, :], axis=2)
    d_chosen = gates * (d_gates - jnp.sum(gates * d_gates, axis=1, keepdims=True))
    d_logits = jnp.sum(picked * d_chosen[:, :, None], axis=1)
    d_moe = (
        d_moe
        + jnp.dot(d_logits, w_router.T, precision=HIGH)
        + d_mixing[:, None] * w_sigmoid[None, :]
    )
    d_router_part = jnp.dot(d_logits.T, moe_wide, precision=HIGH)
    d_sigmoid_part = jnp.dot(d_mixing, moe_wide, precision=HIGH)
    d_middle_norm, d_moe_gain_part = norm_back(middle, inv_two, moe_gain, d_moe)
    d_middle = upstream + d_middle_norm
    small_sums = butterfly(
        jnp.concatenate([d_router_part, d_sigmoid_part[None], d_moe_gain_part[None]], axis=0),
        jnp.add,
        ("tensor", "dp"),
    )
    d_expert_gate = group_scatter(times_first(column, d_gate_e).astype(low), 0)
    d_expert_up = group_scatter(times_first(column, d_up_e).astype(low), 0)
    d_expert_down = group_scatter(times_first(hidden_e, upstream_column).astype(low), 1)
    d_shared_gate, d_shared_up = spread_in_back(
        (times_first(column, d_gate_s).astype(low), times_first(column, d_up_s).astype(low)),
        *shared_gate.shape,
    )
    d_shared_down = spread_out_back(
        times_first(hidden_s, upstream_column).astype(low), *shared_down.shape
    )
    whole_middle = group_gather(d_middle.astype(low), 0)
    d_w_output = column_scatter(times_first(attended, whole_middle), 1)
    d_attended = times_last(whole_middle, out_weight).astype(low).reshape(seq_len, -1, DH)
    d_queries, d_keys, d_values = attention_backward(
        queries, keys_in, values_in, d_attended, log_totals, length, factor
    )
    d_projected = jnp.concatenate([d_queries, d_keys, d_values], axis=1)
    d_in_weights = column_scatter(times_first(gathered_one, d_projected), 0)
    d_normed = group_scatter(times_last(d_projected, in_weights).astype(low), 0)
    d_inputs_norm, d_attn_gain_part = norm_back(inputs, inv_one, attn_gain, d_normed)
    d_tokens = d_middle + d_inputs_norm
    d_attn_gain = butterfly(d_attn_gain_part.reshape(-1, 128), jnp.add, ("tensor", "dp")).reshape(-1)
    clip_scale = jnp.sqrt(CLIP_LIMIT / jnp.maximum(peaks, CLIP_LIMIT))
    columns = jnp.repeat(clip_scale, DH)
    query_clipped = (w_query.astype(jnp.float32) * columns[None, :]).astype(low)
    key_clipped = (w_key.astype(jnp.float32) * columns[None, :]).astype(low)
    return (
        combined.astype(low),
        d_tokens,
        d_attn_gain,
        d_in_weights[:, :width],
        d_in_weights[:, width : 2 * width],
        d_in_weights[:, 2 * width :],
        d_w_output,
        small_sums[experts + 1],
        small_sums[:experts].T,
        small_sums[experts],
        d_shared_gate,
        d_shared_up,
        d_shared_down,
        d_expert_gate[None],
        d_expert_up[None],
        d_expert_down[None],
        clip_scale,
        query_clipped,
        key_clipped,
    )


def solution(mesh):
    placed = (
        P(("dp", "tensor"), None),
        P("dp"),
        P(("dp", "tensor"), None),
        P(),
        P("dp", "tensor"),
        P("dp", "tensor"),
        P("dp", "tensor"),
        P("tensor", "dp"),
        P(),
        P(),
        P(),
        P("dp", "tensor"),
        P("dp", "tensor"),
        P("tensor", "dp"),
        P("dp", "tensor", None),
        P("dp", "tensor", None),
        P("dp", None, "tensor"),
        P(("dp", "tensor"), None),
    )
    return jax.shard_map(
        local,
        mesh=mesh,
        in_specs=placed,
        out_specs=(
            P(("dp", "tensor"), None),
            P(("dp", "tensor"), None),
            P(),
            P("dp", "tensor"),
            P("dp", "tensor"),
            P("dp", "tensor"),
            P("tensor", "dp"),
            P(),
            P(),
            P(),
            P("dp", "tensor"),
            P("dp", "tensor"),
            P("tensor", "dp"),
            P("dp", "tensor", None),
            P("dp", "tensor", None),
            P("dp", None, "tensor"),
            P("tensor"),
            P("dp", "tensor"),
            P("dp", "tensor"),
        ),
        check_vma=False,
    )
```

```python
import functools

import jax
import jax.numpy as jnp
from jax import lax
from jax.experimental import pallas as pl
from jax.experimental.pallas import tpu as pltpu
from jax.sharding import PartitionSpec as P

DH = 128


EPS = 1e-06
CLIP_LIMIT = 6.0
NEG = -1e30
HIGH = lax.Precision.HIGHEST
CONTRACT_LAST = (((1,), (1,)), ((), ()))
CONTRACT_FIRST = (((0,), (0,)), ((), ()))


def norm_rows(inputs, gain):
    factor = lax.rsqrt(jnp.mean(inputs * inputs, axis=-1, keepdims=True) + EPS)
    return (inputs * factor * gain, factor)


def norm_back(inputs, factor, gain, upstream):
    scaled = upstream * gain
    inner = jnp.mean(scaled * inputs, axis=-1, keepdims=True)
    return (
        factor * scaled - inputs * (factor * factor * factor) * inner,
        jnp.sum(upstream * inputs * factor, axis=0),
    )


def pairs(count, bit):
    return [(index, index ^ bit) for index in range(count)]


def swap(values_in, bit, axis_name="tensor"):
    return lax.ppermute(values_in, axis_name, pairs(lax.axis_size(axis_name), bit))


def halves(values_in, axis):
    middle_at = values_in.shape[axis] // 2
    return (
        lax.slice_in_dim(values_in, 0, middle_at, axis=axis),
        lax.slice_in_dim(values_in, middle_at, values_in.shape[axis], axis=axis),
    )


def after(value, *others):
    return lax.optimization_barrier((value, others))[0]


def cut_of(block):
    return 1 if block.ndim > 2 else 0


def gather_near(block):
    if lax.axis_size("tensor") != 4:
        return (block,)
    return (block, swap(block, 1), swap(block, 2))


def gather_far(parts):
    if len(parts) == 1:
        return parts
    block, across, along = parts
    cut = cut_of(block)
    first, _ = halves(along, cut)
    _, second = halves(across, cut)
    return (block, across, along, swap(first, 1), swap(second, 2))


def gather_join(parts, axis):
    if len(parts) == 1:
        return lax.all_gather(parts[0], "tensor", axis=axis, tiled=True)
    block, across, along, first, second = parts
    diagonal = jnp.concatenate([first, second], axis=cut_of(block))
    here = lax.axis_index("tensor")
    odd, high = (here & 1) == 1, (here & 2) == 2
    low_even, low_odd = jnp.where(odd, across, block), jnp.where(odd, block, across)
    high_even, high_odd = jnp.where(odd, diagonal, along), jnp.where(odd, along, diagonal)
    return jnp.concatenate(
        [
            jnp.where(high, high_even, low_even),
            jnp.where(high, high_odd, low_odd),
            jnp.where(high, low_even, high_even),
            jnp.where(high, low_odd, high_odd),
        ],
        axis=axis,
    )


def block_of(partial, other, axis):
    size = partial.shape[axis] // 4
    return lax.dynamic_slice_in_dim(
        partial, (lax.axis_index("tensor") ^ other) * size, size, axis
    )


def scatter_far(partial, axis):
    if lax.axis_size("tensor") != 4:
        return (partial,)
    first, second = halves(block_of(partial, 3, axis), cut_of(partial))
    return (partial, swap(first, 1), swap(second, 2))


def scatter_ready(parts, axis):
    if len(parts) == 1:
        return parts
    partial, over_x, over_y = parts
    cut = cut_of(partial)
    wide = jnp.float32
    near_y, near_x = halves(block_of(partial, 2, axis), cut), halves(block_of(partial, 1, axis), cut)
    send_y = jnp.concatenate(
        [(near_y[0].astype(wide) + over_x.astype(wide)).astype(partial.dtype), near_y[1]], axis=cut
    )
    send_x = jnp.concatenate(
        [near_x[0], (near_x[1].astype(wide) + over_y.astype(wide)).astype(partial.dtype)], axis=cut
    )
    return (block_of(partial, 0, axis), send_y, send_x)


def scatter_send(parts, axis):
    if len(parts) == 1:
        return (lax.psum_scatter(parts[0], "tensor", scatter_dimension=axis, tiled=True),)
    block, send_y, send_x = parts
    return (block, swap(send_y, 2), swap(send_x, 1))


def scatter_near(parts, axis):
    return scatter_send(scatter_ready(parts, axis), axis)


def scatter_sum(parts):
    total = parts[0].astype(jnp.float32)
    for part in parts[1:]:
        total = total + part.astype(jnp.float32)
    return total


def column_gather(rows):
    return lax.all_gather(rows, "dp", axis=0, tiled=True)


def column_scatter(partial, axis):
    return lax.psum_scatter(
        partial.astype(jnp.bfloat16), "dp", scatter_dimension=axis, tiled=True
    ).astype(jnp.float32)


def trade(blocks, axis_name):
    return lax.all_to_all(blocks, axis_name, split_axis=0, concat_axis=0, tiled=True)


def butterfly(values_in, combine, axis_names):
    for axis_name in axis_names:
        bit = 1
        while bit < lax.axis_size(axis_name):
            values_in = combine(values_in, swap(values_in, bit, axis_name))
            bit *= 2
    return values_in


def times(left, right):
    return jnp.dot(left, right, preferred_element_type=jnp.float32)


def times_last(left, right):
    return lax.dot_general(left, right, CONTRACT_LAST, preferred_element_type=jnp.float32)


def times_first(left, right):
    return lax.dot_general(left, right, CONTRACT_FIRST, preferred_element_type=jnp.float32)


def slice_width(hidden_width, share):
    return -(-hidden_width // (128 * share)) * 128


def pack(blocks, width):
    *lead, rows, columns = blocks.shape
    groups = width // columns
    blocks = blocks.reshape(*lead, groups, rows // groups, columns)
    return jnp.swapaxes(blocks, -3, -2).reshape(*lead, rows // groups, width)


def unpack(blocks, columns):
    *lead, rows, width = blocks.shape
    groups = width // columns
    blocks = jnp.swapaxes(blocks.reshape(*lead, rows, groups, columns), -3, -2)
    return blocks.reshape(*lead, groups * rows, columns)


def shared_sizes(rows, hidden_width):
    count, owners = lax.axis_size("tensor"), lax.axis_size("dp")
    share = owners // count
    width = slice_width(hidden_width, share)
    return count, share, width, rows // count, width // count


def shared_spread(in_weights, out_weight):
    rows, hidden_width = in_weights[0].shape
    count, share, width, piece, slab = shared_sizes(rows, hidden_width)
    extra = share * width - hidden_width
    padded = [jnp.pad(w, ((0, 0), (0, extra))).reshape(count, piece, -1) for w in in_weights]
    first = jnp.stack(
        [
            jnp.concatenate([w[:, :, s * width : (s + 1) * width] for w in padded], axis=2)
            for s in range(share)
        ],
        axis=1,
    )
    last = jnp.pad(out_weight, ((0, extra), (0, 0)))
    last = pack(last.reshape(share, count, slab, -1).transpose(1, 0, 2, 3), 2 * width)
    return trade(jnp.concatenate([first, last], axis=2), "tensor")


def shared_owners(blocks):
    count, share, rows, width = blocks.shape
    return trade(blocks.reshape(count * share, rows, width), "dp")


def shared_join(whole, rows, columns):
    count, owners, _, width = whole.shape
    piece = rows // count
    first = whole[:, :, :piece].transpose(1, 0, 2, 3).reshape(owners * rows, width)
    last = unpack(whole[:, :, piece:], columns).transpose(0, 2, 1, 3)
    return first, last.reshape(-1, owners * columns)


def shared_back(grad_in, grad_out, columns):
    count, owners = lax.axis_size("tensor"), lax.axis_size("dp")
    rows, width = grad_in.shape
    first = grad_in.reshape(owners, count, rows // (owners * count), width).transpose(1, 0, 2, 3)
    last = grad_out.reshape(count, -1, owners, columns).transpose(0, 2, 1, 3)
    return jnp.concatenate([first, pack(last, width)], axis=2)


def shared_back_group(blocks, rows, columns, hidden_width):
    count, share, width, piece, slab = shared_sizes(rows, hidden_width)
    blocks = trade(blocks.reshape(count, share, -1, 2 * width), "tensor")
    first = blocks[:, :, :piece].reshape(count, share, piece, 2, width)
    first = [
        jnp.concatenate([first[:, s, :, part] for s in range(share)], axis=2)
        .reshape(rows, share * width)[:, :hidden_width]
        .astype(jnp.float32)
        for part in range(2)
    ]
    last = unpack(blocks[:, :, piece:], columns).transpose(1, 0, 2, 3).reshape(-1, columns)
    return first[0], first[1], last[:hidden_width].astype(jnp.float32)


def join_kernel(place_ref, *refs):
    count = (len(refs) - 2) // 5
    whole, sems = refs[-2:]
    here = place_ref[0]
    copies = []
    for side in range(count):
        parts = refs[5 * side : 5 * side + 5]
        rows, columns = parts[0].shape
        half = rows // 2
        for index, (part, other, shift) in enumerate(
            zip(parts, (0, 1, 2, 3, 3), (0, 0, 0, 0, half))
        ):
            start = pl.multiple_of((here ^ other) * rows + shift, half)
            copies.append(
                pltpu.make_async_copy(
                    part,
                    whole.at[pl.ds(start, part.shape[0]), pl.ds(side * columns, columns)],
                    sems.at[5 * side + index],
                )
            )
    for copy in copies:
        copy.start()
    for copy in copies:
        copy.wait()


def gather_rows(*gathers):
    if len(gathers[0]) == 1:
        return jnp.concatenate([gather_join(parts, 0) for parts in gathers], axis=1)
    rows, columns = gathers[0][0].shape
    shape = (4 * rows, len(gathers) * columns)
    operands = [part for parts in gathers for part in parts]
    return pl.pallas_call(
        join_kernel,
        grid_spec=pltpu.PrefetchScalarGridSpec(
            num_scalar_prefetch=1,
            grid=(1,),
            in_specs=[pl.BlockSpec(memory_space=pl.ANY)] * len(operands),
            out_specs=pl.BlockSpec(shape, lambda step, _: (0, 0)),
            scratch_shapes=[pltpu.SemaphoreType.DMA((len(operands),))],
        ),
        out_shape=jax.ShapeDtypeStruct(shape, operands[0].dtype),
        compiler_params=pltpu.CompilerParams(vmem_limit_bytes=40 << 20),
        name="join_rows",
    )(lax.axis_index("tensor").astype(jnp.int32).reshape(1), *operands)


def attention_scores(query_block, keys_in, start, length):
    rows, columns = query_block.shape[0], keys_in.shape[0]
    raw = lax.dot_general(
        query_block, keys_in, CONTRACT_LAST, preferred_element_type=jnp.float32
    ) * DH ** (-0.5)
    row = start + lax.broadcasted_iota(jnp.int32, (rows, columns), 0)
    column = lax.broadcasted_iota(jnp.int32, (rows, columns), 1)
    allowed = (column <= row) & (column < length)
    scores = jnp.where(allowed, raw, NEG)
    powers = jnp.exp(scores - jnp.max(scores, axis=1, keepdims=True))
    probs = powers * (1.0 / jnp.sum(powers, axis=1, keepdims=True))
    return (scores, row, probs)


def attention_forward_kernel(
    length_ref, query_ref, key_ref, value_ref, attended_ref, peak_ref, *, block_len
):
    length = length_ref[0]
    peak = jnp.full((1, 1), NEG, jnp.float32)
    for start in range(0, query_ref.shape[0], block_len):
        stop = start + block_len
        scores, row, probs = attention_scores(
            query_ref[start:stop, :], key_ref[:stop, :], start, length
        )
        attended_ref[start:stop, :] = jnp.dot(
            probs.astype(jnp.bfloat16), value_ref[:stop, :], preferred_element_type=jnp.float32
        ).astype(jnp.bfloat16)
        counted = jnp.where(row < length, scores, NEG)
        peak = jnp.maximum(
            peak, jnp.max(jnp.max(counted, axis=1, keepdims=True), axis=0, keepdims=True)
        )
    peak_ref[0] = jnp.broadcast_to(peak, peak_ref.shape[1:])


def attention_forward(projected, length):
    seq_len = projected.shape[0]
    heads = projected.shape[1] // (3 * DH)
    block_len = min(256, seq_len)

    def columns(part):
        return pl.BlockSpec((seq_len, DH), lambda head, _: (0, part * heads + head))

    attended, peaks = pl.pallas_call(
        functools.partial(attention_forward_kernel, block_len=block_len),
        grid_spec=pltpu.PrefetchScalarGridSpec(
            num_scalar_prefetch=1,
            grid=(heads,),
            in_specs=[columns(0), columns(1), columns(2)],
            out_specs=[
                pl.BlockSpec((seq_len, DH), lambda head, _: (0, head)),
                pl.BlockSpec((1, 8, 128), lambda head, _: (head, 0, 0)),
            ],
        ),
        out_shape=(
            jax.ShapeDtypeStruct((seq_len, heads * DH), jnp.bfloat16),
            jax.ShapeDtypeStruct((heads, 8, 128), jnp.float32),
        ),
        compiler_params=pltpu.CompilerParams(vmem_limit_bytes=48 << 20),
        cost_estimate=pl.CostEstimate(
            flops=6 * heads * seq_len * seq_len * DH,
            bytes_accessed=8 * heads * seq_len * DH,
            transcendentals=heads * seq_len * seq_len,
        ),
        name="attention_forward",
    )(length, projected, projected, projected)
    return (attended, peaks[:, 0, 0])


def attention_backward_kernel(
    length_ref, query_ref, key_ref, value_ref, grad_ref, out_ref, key_sum, value_sum, *, block_len
):
    part = pl.program_id(1)
    low, factor = jnp.bfloat16, DH ** (-0.5)

    @pl.when(part == 0)
    def _():
        length = length_ref[0]
        seq_len = query_ref.shape[0]
        for start in range(seq_len - block_len, -1, -block_len):
            stop = start + block_len
            query_block, grad_block = query_ref[start:stop, :], grad_ref[start:stop, :]
            keys_in = key_ref[:stop, :]
            _, _, probs = attention_scores(query_block, keys_in, start, length)
            along = lax.dot_general(
                grad_block, value_ref[:stop, :], CONTRACT_LAST, preferred_element_type=jnp.float32
            )
            inner = jnp.sum(probs * along, axis=1, keepdims=True)
            grad_scores = (probs * (along - inner)).astype(low)
            out_ref[start:stop, :] = (
                jnp.dot(grad_scores, keys_in, preferred_element_type=jnp.float32) * factor
            ).astype(low)
            key_part = lax.dot_general(
                grad_scores, query_block, CONTRACT_FIRST, preferred_element_type=jnp.float32
            )
            value_part = lax.dot_general(
                probs.astype(low), grad_block, CONTRACT_FIRST, preferred_element_type=jnp.float32
            )
            if stop == seq_len:
                key_sum[...] = key_part
                value_sum[...] = value_part
            else:
                key_sum[:stop, :] += key_part
                value_sum[:stop, :] += value_part

    @pl.when(part == 1)
    def _():
        out_ref[...] = (key_sum[...] * factor).astype(low)

    @pl.when(part == 2)
    def _():
        out_ref[...] = value_sum[...].astype(low)


def attention_backward(projected, grad_out, length):
    seq_len = projected.shape[0]
    heads = projected.shape[1] // (3 * DH)
    block_len = min(256, seq_len)

    def columns(part):
        return pl.BlockSpec((seq_len, DH), lambda head, _, __: (0, part * heads + head))

    return pl.pallas_call(
        functools.partial(attention_backward_kernel, block_len=block_len),
        grid_spec=pltpu.PrefetchScalarGridSpec(
            num_scalar_prefetch=1,
            grid=(heads, 3),
            in_specs=[
                columns(0),
                columns(1),
                columns(2),
                pl.BlockSpec((seq_len, DH), lambda head, _, __: (0, head)),
            ],
            out_specs=pl.BlockSpec((seq_len, DH), lambda head, part, _: (0, part * heads + head)),
            scratch_shapes=[
                pltpu.VMEM((seq_len, DH), jnp.float32),
                pltpu.VMEM((seq_len, DH), jnp.float32),
            ],
        ),
        out_shape=jax.ShapeDtypeStruct(projected.shape, jnp.bfloat16),
        compiler_params=pltpu.CompilerParams(vmem_limit_bytes=48 << 20),
        cost_estimate=pl.CostEstimate(
            flops=12 * heads * seq_len * seq_len * DH,
            bytes_accessed=14 * heads * seq_len * DH,
            transcendentals=heads * seq_len * seq_len,
        ),
        name="attention_backward",
    )(length, projected, projected, projected, grad_out)


def expert_backward_kernel(
    scale_ref,
    upstream_ref,
    *refs,
):
    low = jnp.bfloat16
    count = 2
    pre_refs, in_refs, out_refs = refs[:count], refs[count : 2 * count], refs[2 * count : 3 * count]
    grad_refs = refs[3 * count : 4 * count]
    hidden_refs = refs[4 * count : 5 * count]
    inner_ref, rows_ref = refs[5 * count :]
    upstream = upstream_ref[...]
    total = None
    inners = []
    for part in range(count):
        width = hidden_refs[part].shape[1]
        scale = scale_ref[:, part : part + 1]
        gate_pre = pre_refs[part][:, :width].astype(jnp.float32)
        up_pre = pre_refs[part][:, width:].astype(jnp.float32)
        raw = lax.dot_general(
            upstream, out_refs[part][...], CONTRACT_LAST, preferred_element_type=jnp.float32
        )
        sigma = 1.0 / (1.0 + jnp.exp(-gate_pre))
        activated = gate_pre * sigma
        hidden = activated * up_pre
        inners.append(jnp.sum(hidden * raw, axis=1, keepdims=True))
        scaled = raw * scale
        hidden_refs[part][...] = (hidden * scale).astype(low)
        grad_refs[part][:, :width] = (
            scaled * up_pre * (sigma * (1.0 + gate_pre * (1.0 - sigma)))
        ).astype(low)
        grad_refs[part][:, width:] = (scaled * activated).astype(low)
        rows = lax.dot_general(
            grad_refs[part][...], in_refs[part][...], CONTRACT_LAST, preferred_element_type=jnp.float32
        )
        total = rows if total is None else total + rows
    inner_ref[...] = jnp.concatenate(inners, axis=1)
    rows_ref[...] = total.astype(low)


def expert_backward(scales, upstream, pre, in_weights, out_weights):
    rows, model_width = upstream.shape
    block = min(256, rows)
    widths = [w.shape[0] for w in out_weights]
    low = jnp.bfloat16

    def tall(width):
        return pl.BlockSpec((block, width), lambda step: (step, 0))

    def whole(array):
        return pl.BlockSpec(array.shape, lambda step: (0, 0), pipeline_mode=pl.Buffered(1))

    outs = pl.pallas_call(
        expert_backward_kernel,
        grid=(rows // block,),
        in_specs=[tall(2), tall(model_width)]
        + [tall(2 * w) for w in widths]
        + [whole(w) for w in in_weights]
        + [whole(w) for w in out_weights],
        out_specs=[tall(2 * w) for w in widths]
        + [tall(w) for w in widths]
        + [tall(2), tall(model_width)],
        out_shape=[jax.ShapeDtypeStruct((rows, 2 * w), low) for w in widths]
        + [jax.ShapeDtypeStruct((rows, w), low) for w in widths]
        + [
            jax.ShapeDtypeStruct((rows, 2), jnp.float32),
            jax.ShapeDtypeStruct((rows, model_width), low),
        ],
        compiler_params=pltpu.CompilerParams(vmem_limit_bytes=60 << 20),
        cost_estimate=pl.CostEstimate(
            flops=6 * rows * model_width * sum(widths),
            bytes_accessed=2 * rows * (2 * model_width + 5 * sum(widths))
            + 6 * model_width * sum(widths),
            transcendentals=rows * sum(widths),
        ),
        name="expert_backward",
    )(scales, upstream, *pre, *in_weights, *out_weights)
    return outs[0:2], outs[2:4], outs[4], outs[5]


def local(
    tokens,
    lengths,
    routes,
    attn_gain,
    w_query,
    w_key,
    w_value,
    w_output,
    moe_gain,
    w_router,
    w_sigmoid,
    shared_gate,
    shared_up,
    shared_down,
    expert_gate,
    expert_up,
    expert_down,
    cotangent,
):
    low = jnp.bfloat16
    hold = lax.optimization_barrier
    inputs = tokens.astype(jnp.float32)
    normed, inv_one = norm_rows(inputs, attn_gain)
    width = w_query.shape[1]
    hidden_width = expert_gate.shape[2]
    shared_shape = (shared_gate.shape[0], shared_down.shape[1], shared_gate.shape[1])
    in_weights = column_gather(jnp.concatenate([w_query, w_key, w_value], axis=1))
    out_weight = lax.all_gather(w_output, "dp", axis=1, tiled=True)
    upstream_column = column_gather(cotangent)
    normed_parts = gather_far(gather_near(normed.astype(low)))
    shared_blocks = shared_spread((shared_gate, shared_up), shared_down)
    normed_parts, expert_gate = hold((normed_parts, expert_gate))
    gathered_one = gather_join(normed_parts, 0)
    gate_parts = gather_near(expert_gate[0])
    projected = times(gathered_one, in_weights).astype(low)
    projected, shared_blocks, gate_parts, expert_up = hold(
        (projected, shared_blocks, gate_parts, expert_up)
    )
    up_parts = gather_near(expert_up[0])
    shared_blocks = shared_owners(shared_blocks)[None]
    attended, peaks = attention_forward(projected, lengths)
    middle_parts = scatter_near(scatter_far(times(attended, out_weight).astype(low), 0), 0)
    middle_parts, gate_parts, up_parts, shared_blocks, peaks = hold(
        (middle_parts, gate_parts, up_parts, shared_blocks, peaks)
    )
    gate_parts, up_parts = gather_far(gate_parts), gather_far(up_parts)
    middle = inputs + scatter_sum(middle_parts)
    moe_norm, inv_two = norm_rows(middle, moe_gain)
    moe_low, shared_blocks, peaks = hold((moe_norm.astype(low), shared_blocks, peaks))
    column = column_gather(moe_low)
    gate_parts, up_parts, expert_down, shared_blocks = hold(
        (gate_parts, up_parts, expert_down, shared_blocks)
    )
    shared_parts = gather_near(shared_blocks)
    down_parts = gather_near(expert_down[0])
    full_in = gather_rows(gate_parts, up_parts)
    moe_wide = moe_low.astype(jnp.float32)
    experts = w_router.shape[1]
    owners = lax.axis_size("dp")
    rows_dev, route_count = routes.shape
    column_rows = owners * rows_dev
    logits = jnp.dot(moe_wide, w_router, precision=HIGH)
    picked = (routes[:, :, None] == jnp.arange(experts, dtype=jnp.int32)[None, None, :]).astype(
        jnp.float32
    )
    chosen = jnp.sum(picked * logits[:, None, :], axis=2)
    gates = jax.nn.softmax(chosen, axis=1)
    mixing = jax.nn.sigmoid(jnp.dot(moe_wide, w_sigmoid, precision=HIGH))
    gate_of = jnp.sum(picked * gates[:, :, None], axis=1)
    scales = jnp.stack([gate_of.T, jnp.broadcast_to(mixing[None], (experts, rows_dev))], axis=1)
    scales = trade(scales, "dp").transpose(0, 2, 1).reshape(column_rows, 2)
    peaks = butterfly(peaks, jnp.maximum, ("dp",))
    column, full_in, scales, peaks, shared_parts = hold(
        (column, full_in, scales, peaks, shared_parts)
    )
    shared_parts = gather_far(shared_parts)
    pre_e = times(column, full_in).astype(low)
    pre_e, shared_parts, down_parts = hold((pre_e, shared_parts, down_parts))
    down_parts = gather_far(down_parts)
    part_in, part_down = shared_join(gather_join(shared_parts, 0), *shared_shape[:2])
    full_down = gather_join(down_parts, 1)
    pre_s = times(column, part_in).astype(low)
    (d_pre_e, d_pre_s), (hidden_e, hidden_s), inner, d_rows = expert_backward(
        scales, upstream_column, (pre_e, pre_s), (full_in, part_in), (full_down, part_down)
    )
    d_moe = column_scatter(d_rows, 0)
    inner = trade(inner.reshape(owners, rows_dev, 2).transpose(0, 2, 1), "dp")
    grad_down_e = times_first(hidden_e, upstream_column).astype(low)
    grad_down_e, d_pre_s, hidden_s = hold((grad_down_e, d_pre_s, hidden_s))
    back_down_e = scatter_far(grad_down_e, 1)
    grad_down_s = times_first(hidden_s, upstream_column).astype(low)
    grad_in_s = times_first(column, d_pre_s).astype(low)
    back_down_e, grad_down_s, grad_in_s, hidden_e, hidden_s = hold(
        (back_down_e, grad_down_s, grad_in_s, hidden_e, hidden_s)
    )
    back_down_e = scatter_near(back_down_e, 1)
    grads_s = shared_back(grad_in_s, grad_down_s, shared_shape[1])
    hidden_e, hidden_s, grads_s = hold((hidden_e, hidden_s, grads_s))
    back_s = scatter_far(grads_s, 0)
    routed_rows = (times(hidden_e, full_down) + times(hidden_s, part_down)).astype(low)
    routed_rows, back_s, inner, back_down_e = hold((routed_rows, back_s, inner, back_down_e))
    routed = column_scatter(routed_rows, 0)
    upstream = cotangent.astype(jnp.float32)
    d_mixing = mixing * (1.0 - mixing) * jnp.sum(inner[:, 1], axis=0)
    d_gates = jnp.sum(picked * inner[:, 0].T[:, None, :], axis=2)
    d_chosen = gates * (d_gates - jnp.sum(gates * d_gates, axis=1, keepdims=True))
    d_logits = jnp.sum(picked * d_chosen[:, :, None], axis=1)
    d_router_part = jnp.dot(d_logits.T, moe_wide, precision=HIGH)
    d_sigmoid_part = jnp.dot(d_mixing, moe_wide, precision=HIGH)
    d_moe = (
        d_moe
        + jnp.dot(d_logits, w_router.T, precision=HIGH)
        + d_mixing[:, None] * w_sigmoid[None, :]
    )
    d_middle_norm, d_moe_gain_part = norm_back(middle, inv_two, moe_gain, d_moe)
    d_middle = upstream + d_middle_norm
    d_middle_low, back_s, d_pre_e = hold((d_middle.astype(low), back_s, d_pre_e))
    whole_parts = gather_near(d_middle_low)
    back_s = scatter_ready(back_s, 0)
    whole_parts, back_s = hold((whole_parts, back_s))
    whole_parts = gather_far(whole_parts)
    whole_parts, back_s = hold((whole_parts, back_s))
    back_s = scatter_send(back_s, 0)
    whole_middle = gather_join(whole_parts, 0)
    d_attended = times_last(whole_middle, out_weight).astype(low)
    d_projected = attention_backward(projected, d_attended, lengths)
    small_parts = jnp.concatenate(
        [d_router_part, d_sigmoid_part[None], d_moe_gain_part[None]], axis=0
    )
    d_w_output = column_scatter(times_first(attended, whole_middle), 1)
    d_normed_rows = times_last(d_projected, in_weights).astype(low)
    d_normed_rows, d_projected, small_parts = hold((d_normed_rows, d_projected, small_parts))
    normed_parts = scatter_far(d_normed_rows, 0)
    d_in_weights = column_scatter(times_first(gathered_one, d_projected), 0)
    normed_parts, back_s, d_pre_e, back_down_e = hold(
        (normed_parts, back_s, d_pre_e, back_down_e)
    )
    normed_parts = scatter_near(normed_parts, 0)
    back_s = trade(scatter_sum(back_s).astype(low)[0], "dp")
    grad_gate_up = times_first(column, d_pre_e).astype(low)
    normed_parts, grad_gate_up = hold((normed_parts, grad_gate_up))
    d_expert_down = scatter_sum(back_down_e)
    back_gate_up = scatter_ready(scatter_far(grad_gate_up, 0), 0)
    d_normed = scatter_sum(normed_parts)
    d_inputs_norm, d_attn_gain_part = norm_back(inputs, inv_one, attn_gain, d_normed)
    small_sums = butterfly(
        jnp.concatenate([small_parts, d_attn_gain_part[None]], axis=0), jnp.add, ("tensor",)
    )
    back_gate_up, d_expert_down, small_sums, routed = hold(
        (back_gate_up, d_expert_down, small_sums, routed)
    )
    back_gate_up = scatter_send(back_gate_up, 0)
    d_tokens = d_middle + d_inputs_norm
    small_sums = butterfly(small_sums, jnp.add, ("dp",))
    d_attn_gain = small_sums[experts + 2]
    d_shared_gate, d_shared_up, d_shared_down = shared_back_group(back_s, *shared_shape)
    d_expert_in = scatter_sum(back_gate_up)
    clip_scale = jnp.sqrt(CLIP_LIMIT / jnp.maximum(peaks, CLIP_LIMIT))
    columns = jnp.repeat(clip_scale, DH)
    query_clipped = (w_query.astype(jnp.float32) * columns[None, :]).astype(low)
    key_clipped = (w_key.astype(jnp.float32) * columns[None, :]).astype(low)
    return (
        (middle + routed).astype(low),
        d_tokens,
        d_attn_gain,
        d_in_weights[:, :width],
        d_in_weights[:, width : 2 * width],
        d_in_weights[:, 2 * width :],
        d_w_output,
        small_sums[experts + 1],
        small_sums[:experts].T,
        small_sums[experts],
        d_shared_gate,
        d_shared_up,
        d_shared_down,
        d_expert_in[None, :, :hidden_width],
        d_expert_in[None, :, hidden_width:],
        d_expert_down[None],
        clip_scale,
        query_clipped,
        key_clipped,
    )


def solution(mesh):
    placed = (
        P(("dp", "tensor"), None),
        P("dp"),
        P(("dp", "tensor"), None),
        P(),
        P("dp", "tensor"),
        P("dp", "tensor"),
        P("dp", "tensor"),
        P("tensor", "dp"),
        P(),
        P(),
        P(),
        P("dp", "tensor"),
        P("dp", "tensor"),
        P("tensor", "dp"),
        P("dp", "tensor", None),
        P("dp", "tensor", None),
        P("dp", None, "tensor"),
        P(("dp", "tensor"), None),
    )
    return jax.shard_map(
        local,
        mesh=mesh,
        in_specs=placed,
        out_specs=(
            P(("dp", "tensor"), None),
            P(("dp", "tensor"), None),
            P(),
            P("dp", "tensor"),
            P("dp", "tensor"),
            P("dp", "tensor"),
            P("tensor", "dp"),
            P(),
            P(),
            P(),
            P("dp", "tensor"),
            P("dp", "tensor"),
            P("tensor", "dp"),
            P("dp", "tensor", None),
            P("dp", "tensor", None),
            P("dp", None, "tensor"),
            P("tensor"),
            P("dp", "tensor"),
            P("dp", "tensor"),
        ),
        check_vma=False,
    )
```

```python
import functools

import jax
import jax.numpy as jnp
from jax import lax
from jax.experimental import pallas as pl
from jax.experimental.pallas import tpu as pltpu
from jax.sharding import PartitionSpec as P

DH = 128


EPS = 1e-06
CLIP_LIMIT = 6.0
NEG = -1e30
HIGH = lax.Precision.HIGHEST
CONTRACT_LAST = (((1,), (1,)), ((), ()))
CONTRACT_FIRST = (((0,), (0,)), ((), ()))


def norm_rows(inputs, gain):
    factor = lax.rsqrt(jnp.mean(inputs * inputs, axis=-1, keepdims=True) + EPS)
    return (inputs * factor * gain, factor)


def norm_back(inputs, factor, gain, upstream):
    scaled = upstream * gain
    inner = jnp.mean(scaled * inputs, axis=-1, keepdims=True)
    return (
        factor * scaled - inputs * (factor * factor * factor) * inner,
        jnp.sum(upstream * inputs * factor, axis=0),
    )


def pairs(count, bit):
    return [(index, index ^ bit) for index in range(count)]


def swap(values_in, bit, axis_name="tensor"):
    return lax.ppermute(values_in, axis_name, pairs(lax.axis_size(axis_name), bit))


def halves(values_in, axis):
    middle_at = values_in.shape[axis] // 2
    return (
        lax.slice_in_dim(values_in, 0, middle_at, axis=axis),
        lax.slice_in_dim(values_in, middle_at, values_in.shape[axis], axis=axis),
    )


def after(value, *others):
    return lax.optimization_barrier((value, others))[0]


def cut_of(block):
    return 1 if block.ndim > 2 else 0


def gather_near(block):
    if lax.axis_size("tensor") != 4:
        return (block,)
    return (block, swap(block, 1), swap(block, 2))


def gather_far(parts):
    if len(parts) == 1:
        return parts
    block, across, along = parts
    cut = cut_of(block)
    first, _ = halves(along, cut)
    _, second = halves(across, cut)
    return (block, across, along, swap(first, 1), swap(second, 2))


def gather_join(parts, axis):
    if len(parts) == 1:
        return lax.all_gather(parts[0], "tensor", axis=axis, tiled=True)
    block, across, along, first, second = parts
    diagonal = jnp.concatenate([first, second], axis=cut_of(block))
    here = lax.axis_index("tensor")
    odd, high = (here & 1) == 1, (here & 2) == 2
    low_even, low_odd = jnp.where(odd, across, block), jnp.where(odd, block, across)
    high_even, high_odd = jnp.where(odd, diagonal, along), jnp.where(odd, along, diagonal)
    return jnp.concatenate(
        [
            jnp.where(high, high_even, low_even),
            jnp.where(high, high_odd, low_odd),
            jnp.where(high, low_even, high_even),
            jnp.where(high, low_odd, high_odd),
        ],
        axis=axis,
    )


def block_of(partial, other, axis):
    size = partial.shape[axis] // 4
    return lax.dynamic_slice_in_dim(
        partial, (lax.axis_index("tensor") ^ other) * size, size, axis
    )


def scatter_far(partial, axis):
    if lax.axis_size("tensor") != 4:
        return (partial,)
    first, second = halves(block_of(partial, 3, axis), cut_of(partial))
    return (partial, swap(first, 1), swap(second, 2))


def scatter_ready(parts, axis):
    if len(parts) == 1:
        return parts
    partial, over_x, over_y = parts
    cut = cut_of(partial)
    wide = jnp.float32
    near_y, near_x = halves(block_of(partial, 2, axis), cut), halves(block_of(partial, 1, axis), cut)
    send_y = jnp.concatenate(
        [(near_y[0].astype(wide) + over_x.astype(wide)).astype(partial.dtype), near_y[1]], axis=cut
    )
    send_x = jnp.concatenate(
        [near_x[0], (near_x[1].astype(wide) + over_y.astype(wide)).astype(partial.dtype)], axis=cut
    )
    return (block_of(partial, 0, axis), send_y, send_x)


def scatter_send(parts, axis):
    if len(parts) == 1:
        return (lax.psum_scatter(parts[0], "tensor", scatter_dimension=axis, tiled=True),)
    block, send_y, send_x = parts
    return (block, swap(send_y, 2), swap(send_x, 1))


def scatter_near(parts, axis):
    return scatter_send(scatter_ready(parts, axis), axis)


def scatter_sum(parts):
    total = parts[0].astype(jnp.float32)
    for part in parts[1:]:
        total = total + part.astype(jnp.float32)
    return total


def column_gather(rows):
    return lax.all_gather(rows, "dp", axis=0, tiled=True)


def column_scatter(partial, axis):
    return lax.psum_scatter(
        partial.astype(jnp.bfloat16), "dp", scatter_dimension=axis, tiled=True
    ).astype(jnp.float32)


def trade(blocks, axis_name):
    return lax.all_to_all(blocks, axis_name, split_axis=0, concat_axis=0, tiled=True)


def butterfly(values_in, combine, axis_names):
    for axis_name in axis_names:
        bit = 1
        while bit < lax.axis_size(axis_name):
            values_in = combine(values_in, swap(values_in, bit, axis_name))
            bit *= 2
    return values_in


def times(left, right):
    return jnp.dot(left, right, preferred_element_type=jnp.float32)


def times_last(left, right):
    return lax.dot_general(left, right, CONTRACT_LAST, preferred_element_type=jnp.float32)


def times_first(left, right):
    return lax.dot_general(left, right, CONTRACT_FIRST, preferred_element_type=jnp.float32)


def slice_width(hidden_width, share):
    return -(-hidden_width // (128 * share)) * 128


def pack(blocks, width):
    *lead, rows, columns = blocks.shape
    groups = width // columns
    blocks = blocks.reshape(*lead, groups, rows // groups, columns)
    return jnp.swapaxes(blocks, -3, -2).reshape(*lead, rows // groups, width)


def unpack(blocks, columns):
    *lead, rows, width = blocks.shape
    groups = width // columns
    blocks = jnp.swapaxes(blocks.reshape(*lead, rows, groups, columns), -3, -2)
    return blocks.reshape(*lead, groups * rows, columns)


def shared_sizes(rows, hidden_width):
    count, owners = lax.axis_size("tensor"), lax.axis_size("dp")
    share = owners // count
    width = slice_width(hidden_width, share)
    return count, share, width, rows // count, width // count


def shared_spread(in_weights, out_weight):
    rows, hidden_width = in_weights[0].shape
    count, share, width, piece, slab = shared_sizes(rows, hidden_width)
    extra = share * width - hidden_width
    padded = [jnp.pad(w, ((0, 0), (0, extra))).reshape(count, piece, -1) for w in in_weights]
    first = jnp.stack(
        [
            jnp.concatenate([w[:, :, s * width : (s + 1) * width] for w in padded], axis=2)
            for s in range(share)
        ],
        axis=1,
    )
    last = jnp.pad(out_weight, ((0, extra), (0, 0)))
    last = pack(last.reshape(share, count, slab, -1).transpose(1, 0, 2, 3), 2 * width)
    return trade(jnp.concatenate([first, last], axis=2), "tensor")


def shared_owners(blocks):
    count, share, rows, width = blocks.shape
    return trade(blocks.reshape(count * share, rows, width), "dp")


def shared_join(whole, rows, columns):
    count, owners, _, width = whole.shape
    piece = rows // count
    first = whole[:, :, :piece].transpose(1, 0, 2, 3).reshape(owners * rows, width)
    last = unpack(whole[:, :, piece:], columns).transpose(0, 2, 1, 3)
    return first, last.reshape(-1, owners * columns)


def shared_back(grad_in, grad_out, columns):
    count, owners = lax.axis_size("tensor"), lax.axis_size("dp")
    rows, width = grad_in.shape
    first = grad_in.reshape(owners, count, rows // (owners * count), width).transpose(1, 0, 2, 3)
    last = grad_out.reshape(count, -1, owners, columns).transpose(0, 2, 1, 3)
    return jnp.concatenate([first, pack(last, width)], axis=2)


def shared_back_group(blocks, rows, columns, hidden_width):
    count, share, width, piece, slab = shared_sizes(rows, hidden_width)
    blocks = trade(blocks.reshape(count, share, -1, 2 * width), "tensor")
    first = blocks[:, :, :piece].reshape(count, share, piece, 2, width)
    first = [
        jnp.concatenate([first[:, s, :, part] for s in range(share)], axis=2)
        .reshape(rows, share * width)[:, :hidden_width]
        .astype(jnp.float32)
        for part in range(2)
    ]
    last = unpack(blocks[:, :, piece:], columns).transpose(1, 0, 2, 3).reshape(-1, columns)
    return first[0], first[1], last[:hidden_width].astype(jnp.float32)


def join_kernel(place_ref, *refs):
    count = (len(refs) - 2) // 5
    whole, sems = refs[-2:]
    here = place_ref[0]
    copies = []
    for side in range(count):
        parts = refs[5 * side : 5 * side + 5]
        rows, columns = parts[0].shape
        half = rows // 2
        for index, (part, other, shift) in enumerate(
            zip(parts, (0, 1, 2, 3, 3), (0, 0, 0, 0, half))
        ):
            start = pl.multiple_of((here ^ other) * rows + shift, half)
            copies.append(
                pltpu.make_async_copy(
                    part,
                    whole.at[pl.ds(start, part.shape[0]), pl.ds(side * columns, columns)],
                    sems.at[5 * side + index],
                )
            )
    for copy in copies:
        copy.start()
    for copy in copies:
        copy.wait()


def gather_rows(*gathers):
    if len(gathers[0]) == 1:
        return jnp.concatenate([gather_join(parts, 0) for parts in gathers], axis=1)
    rows, columns = gathers[0][0].shape
    shape = (4 * rows, len(gathers) * columns)
    operands = [part for parts in gathers for part in parts]
    return pl.pallas_call(
        join_kernel,
        grid_spec=pltpu.PrefetchScalarGridSpec(
            num_scalar_prefetch=1,
            grid=(1,),
            in_specs=[pl.BlockSpec(memory_space=pl.ANY)] * len(operands),
            out_specs=pl.BlockSpec(shape, lambda step, _: (0, 0)),
            scratch_shapes=[pltpu.SemaphoreType.DMA((len(operands),))],
        ),
        out_shape=jax.ShapeDtypeStruct(shape, operands[0].dtype),
        compiler_params=pltpu.CompilerParams(vmem_limit_bytes=40 << 20),
        name="join_rows",
    )(lax.axis_index("tensor").astype(jnp.int32).reshape(1), *operands)


def attention_scores(query_block, keys_in, start, length):
    rows, columns = query_block.shape[0], keys_in.shape[0]
    raw = lax.dot_general(
        query_block, keys_in, CONTRACT_LAST, preferred_element_type=jnp.float32
    ) * DH ** (-0.5)
    row = start + lax.broadcasted_iota(jnp.int32, (rows, columns), 0)
    column = lax.broadcasted_iota(jnp.int32, (rows, columns), 1)
    allowed = (column <= row) & (column < length)
    scores = jnp.where(allowed, raw, NEG)
    powers = jnp.exp(scores - jnp.max(scores, axis=1, keepdims=True))
    probs = powers * (1.0 / jnp.sum(powers, axis=1, keepdims=True))
    return (scores, row, probs)


def attention_forward_kernel(
    length_ref, query_ref, key_ref, value_ref, attended_ref, peak_ref, *, block_len
):
    length = length_ref[0]
    peak = jnp.full((1, 1), NEG, jnp.float32)
    for start in range(0, query_ref.shape[0], block_len):
        stop = start + block_len
        scores, row, probs = attention_scores(
            query_ref[start:stop, :], key_ref[:stop, :], start, length
        )
        attended_ref[start:stop, :] = jnp.dot(
            probs.astype(jnp.bfloat16), value_ref[:stop, :], preferred_element_type=jnp.float32
        ).astype(jnp.bfloat16)
        counted = jnp.where(row < length, scores, NEG)
        peak = jnp.maximum(
            peak, jnp.max(jnp.max(counted, axis=1, keepdims=True), axis=0, keepdims=True)
        )
    peak_ref[0] = jnp.broadcast_to(peak, peak_ref.shape[1:])


def attention_forward(projected, length):
    seq_len = projected.shape[0]
    heads = projected.shape[1] // (3 * DH)
    block_len = min(256, seq_len)

    def columns(part):
        return pl.BlockSpec((seq_len, DH), lambda head, _: (0, part * heads + head))

    attended, peaks = pl.pallas_call(
        functools.partial(attention_forward_kernel, block_len=block_len),
        grid_spec=pltpu.PrefetchScalarGridSpec(
            num_scalar_prefetch=1,
            grid=(heads,),
            in_specs=[columns(0), columns(1), columns(2)],
            out_specs=[
                pl.BlockSpec((seq_len, DH), lambda head, _: (0, head)),
                pl.BlockSpec((1, 8, 128), lambda head, _: (head, 0, 0)),
            ],
        ),
        out_shape=(
            jax.ShapeDtypeStruct((seq_len, heads * DH), jnp.bfloat16),
            jax.ShapeDtypeStruct((heads, 8, 128), jnp.float32),
        ),
        compiler_params=pltpu.CompilerParams(vmem_limit_bytes=48 << 20),
        cost_estimate=pl.CostEstimate(
            flops=6 * heads * seq_len * seq_len * DH,
            bytes_accessed=8 * heads * seq_len * DH,
            transcendentals=heads * seq_len * seq_len,
        ),
        name="attention_forward",
    )(length, projected, projected, projected)
    return (attended, peaks[:, 0, 0])


def attention_backward_kernel(
    length_ref, query_ref, key_ref, value_ref, grad_ref, out_ref, key_sum, value_sum, *, block_len
):
    part = pl.program_id(1)
    low, factor = jnp.bfloat16, DH ** (-0.5)

    @pl.when(part == 0)
    def _():
        length = length_ref[0]
        seq_len = query_ref.shape[0]
        for start in range(seq_len - block_len, -1, -block_len):
            stop = start + block_len
            query_block, grad_block = query_ref[start:stop, :], grad_ref[start:stop, :]
            keys_in = key_ref[:stop, :]
            _, _, probs = attention_scores(query_block, keys_in, start, length)
            along = lax.dot_general(
                grad_block, value_ref[:stop, :], CONTRACT_LAST, preferred_element_type=jnp.float32
            )
            inner = jnp.sum(probs * along, axis=1, keepdims=True)
            grad_scores = (probs * (along - inner)).astype(low)
            out_ref[start:stop, :] = (
                jnp.dot(grad_scores, keys_in, preferred_element_type=jnp.float32) * factor
            ).astype(low)
            key_part = lax.dot_general(
                grad_scores, query_block, CONTRACT_FIRST, preferred_element_type=jnp.float32
            )
            value_part = lax.dot_general(
                probs.astype(low), grad_block, CONTRACT_FIRST, preferred_element_type=jnp.float32
            )
            if stop == seq_len:
                key_sum[...] = key_part
                value_sum[...] = value_part
            else:
                key_sum[:stop, :] += key_part
                value_sum[:stop, :] += value_part

    @pl.when(part == 1)
    def _():
        out_ref[...] = (key_sum[...] * factor).astype(low)

    @pl.when(part == 2)
    def _():
        out_ref[...] = value_sum[...].astype(low)


def attention_backward(projected, grad_out, length):
    seq_len = projected.shape[0]
    heads = projected.shape[1] // (3 * DH)
    block_len = min(256, seq_len)

    def columns(part):
        return pl.BlockSpec((seq_len, DH), lambda head, _, __: (0, part * heads + head))

    return pl.pallas_call(
        functools.partial(attention_backward_kernel, block_len=block_len),
        grid_spec=pltpu.PrefetchScalarGridSpec(
            num_scalar_prefetch=1,
            grid=(heads, 3),
            in_specs=[
                columns(0),
                columns(1),
                columns(2),
                pl.BlockSpec((seq_len, DH), lambda head, _, __: (0, head)),
            ],
            out_specs=pl.BlockSpec((seq_len, DH), lambda head, part, _: (0, part * heads + head)),
            scratch_shapes=[
                pltpu.VMEM((seq_len, DH), jnp.float32),
                pltpu.VMEM((seq_len, DH), jnp.float32),
            ],
        ),
        out_shape=jax.ShapeDtypeStruct(projected.shape, jnp.bfloat16),
        compiler_params=pltpu.CompilerParams(vmem_limit_bytes=48 << 20),
        cost_estimate=pl.CostEstimate(
            flops=12 * heads * seq_len * seq_len * DH,
            bytes_accessed=14 * heads * seq_len * DH,
            transcendentals=heads * seq_len * seq_len,
        ),
        name="attention_backward",
    )(length, projected, projected, projected, grad_out)


def expert_backward_kernel(
    scale_ref,
    upstream_ref,
    *refs,
):
    low = jnp.bfloat16
    count = 2
    pre_refs, in_refs, out_refs = refs[:count], refs[count : 2 * count], refs[2 * count : 3 * count]
    grad_refs = refs[3 * count : 4 * count]
    hidden_refs = refs[4 * count : 5 * count]
    inner_ref, rows_ref = refs[5 * count :]
    upstream = upstream_ref[...]
    total = None
    inners = []
    for part in range(count):
        width = hidden_refs[part].shape[1]
        scale = scale_ref[:, part : part + 1]
        gate_pre = pre_refs[part][:, :width].astype(jnp.float32)
        up_pre = pre_refs[part][:, width:].astype(jnp.float32)
        raw = lax.dot_general(
            upstream, out_refs[part][...], CONTRACT_LAST, preferred_element_type=jnp.float32
        )
        sigma = 1.0 / (1.0 + jnp.exp(-gate_pre))
        activated = gate_pre * sigma
        hidden = activated * up_pre
        inners.append(jnp.sum(hidden * raw, axis=1, keepdims=True))
        scaled = raw * scale
        hidden_refs[part][...] = (hidden * scale).astype(low)
        grad_refs[part][:, :width] = (
            scaled * up_pre * (sigma * (1.0 + gate_pre * (1.0 - sigma)))
        ).astype(low)
        grad_refs[part][:, width:] = (scaled * activated).astype(low)
        rows = lax.dot_general(
            grad_refs[part][...], in_refs[part][...], CONTRACT_LAST, preferred_element_type=jnp.float32
        )
        total = rows if total is None else total + rows
    inner_ref[...] = jnp.concatenate(inners, axis=1)
    rows_ref[...] = total.astype(low)


def expert_backward(scales, upstream, pre, in_weights, out_weights):
    rows, model_width = upstream.shape
    block = min(256, rows)
    widths = [w.shape[0] for w in out_weights]
    low = jnp.bfloat16

    def tall(width):
        return pl.BlockSpec((block, width), lambda step: (step, 0))

    def whole(array):
        return pl.BlockSpec(array.shape, lambda step: (0, 0), pipeline_mode=pl.Buffered(1))

    outs = pl.pallas_call(
        expert_backward_kernel,
        grid=(rows // block,),
        in_specs=[tall(2), tall(model_width)]
        + [tall(2 * w) for w in widths]
        + [whole(w) for w in in_weights]
        + [whole(w) for w in out_weights],
        out_specs=[tall(2 * w) for w in widths]
        + [tall(w) for w in widths]
        + [tall(2), tall(model_width)],
        out_shape=[jax.ShapeDtypeStruct((rows, 2 * w), low) for w in widths]
        + [jax.ShapeDtypeStruct((rows, w), low) for w in widths]
        + [
            jax.ShapeDtypeStruct((rows, 2), jnp.float32),
            jax.ShapeDtypeStruct((rows, model_width), low),
        ],
        compiler_params=pltpu.CompilerParams(vmem_limit_bytes=60 << 20),
        cost_estimate=pl.CostEstimate(
            flops=6 * rows * model_width * sum(widths),
            bytes_accessed=2 * rows * (2 * model_width + 5 * sum(widths))
            + 6 * model_width * sum(widths),
            transcendentals=rows * sum(widths),
        ),
        name="expert_backward",
    )(scales, upstream, *pre, *in_weights, *out_weights)
    return outs[0:2], outs[2:4], outs[4], outs[5]


def local(
    tokens,
    lengths,
    routes,
    attn_gain,
    w_query,
    w_key,
    w_value,
    w_output,
    moe_gain,
    w_router,
    w_sigmoid,
    shared_gate,
    shared_up,
    shared_down,
    expert_gate,
    expert_up,
    expert_down,
    cotangent,
):
    low = jnp.bfloat16
    hold = lax.optimization_barrier
    inputs = tokens.astype(jnp.float32)
    normed, inv_one = norm_rows(inputs, attn_gain)
    width = w_query.shape[1]
    hidden_width = expert_gate.shape[2]
    shared_shape = (shared_gate.shape[0], shared_down.shape[1], shared_gate.shape[1])
    in_weights = column_gather(jnp.concatenate([w_query, w_key, w_value], axis=1))
    out_weight = lax.all_gather(w_output, "dp", axis=1, tiled=True)
    upstream_column = column_gather(cotangent)
    normed_parts = gather_far(gather_near(normed.astype(low)))
    shared_blocks = shared_spread((shared_gate, shared_up), shared_down)
    normed_parts, expert_gate = hold((normed_parts, expert_gate))
    gathered_one = gather_join(normed_parts, 0)
    gate_parts = gather_near(expert_gate[0])
    projected = times(gathered_one, in_weights).astype(low)
    projected, shared_blocks, gate_parts, expert_up = hold(
        (projected, shared_blocks, gate_parts, expert_up)
    )
    up_parts = gather_near(expert_up[0])
    shared_blocks = shared_owners(shared_blocks)[None]
    attended, peaks = attention_forward(projected, lengths)
    attended, up_parts = hold((attended, up_parts))
    middle_parts = scatter_near(scatter_far(times(attended, out_weight).astype(low), 0), 0)
    middle_parts, gate_parts, up_parts, shared_blocks, peaks = hold(
        (middle_parts, gate_parts, up_parts, shared_blocks, peaks)
    )
    gate_parts, up_parts = gather_far(gate_parts), gather_far(up_parts)
    middle = inputs + scatter_sum(middle_parts)
    moe_norm, inv_two = norm_rows(middle, moe_gain)
    moe_low, shared_blocks, peaks = hold((moe_norm.astype(low), shared_blocks, peaks))
    column = column_gather(moe_low)
    gate_parts, up_parts, expert_down, shared_blocks = hold(
        (gate_parts, up_parts, expert_down, shared_blocks)
    )
    shared_parts = gather_near(shared_blocks)
    down_parts = gather_near(expert_down[0])
    full_in = gather_rows(gate_parts, up_parts)
    moe_wide = moe_low.astype(jnp.float32)
    experts = w_router.shape[1]
    owners = lax.axis_size("dp")
    rows_dev, route_count = routes.shape
    column_rows = owners * rows_dev
    logits = jnp.dot(moe_wide, w_router, precision=HIGH)
    picked = (routes[:, :, None] == jnp.arange(experts, dtype=jnp.int32)[None, None, :]).astype(
        jnp.float32
    )
    chosen = jnp.sum(picked * logits[:, None, :], axis=2)
    gates = jax.nn.softmax(chosen, axis=1)
    mixing = jax.nn.sigmoid(jnp.dot(moe_wide, w_sigmoid, precision=HIGH))
    gate_of = jnp.sum(picked * gates[:, :, None], axis=1)
    scales = jnp.stack([gate_of.T, jnp.broadcast_to(mixing[None], (experts, rows_dev))], axis=1)
    scales = trade(scales, "dp").transpose(0, 2, 1).reshape(column_rows, 2)
    peaks = butterfly(peaks, jnp.maximum, ("dp",))
    column, full_in, scales, peaks, shared_parts = hold(
        (column, full_in, scales, peaks, shared_parts)
    )
    shared_parts = gather_far(shared_parts)
    pre_e = times(column, full_in).astype(low)
    pre_e, shared_parts, down_parts = hold((pre_e, shared_parts, down_parts))
    down_parts = gather_far(down_parts)
    part_in, part_down = shared_join(gather_join(shared_parts, 0), *shared_shape[:2])
    full_down = gather_join(down_parts, 1)
    pre_s = times(column, part_in).astype(low)
    (d_pre_e, d_pre_s), (hidden_e, hidden_s), inner, d_rows = expert_backward(
        scales, upstream_column, (pre_e, pre_s), (full_in, part_in), (full_down, part_down)
    )
    d_moe = column_scatter(d_rows, 0)
    inner = trade(inner.reshape(owners, rows_dev, 2).transpose(0, 2, 1), "dp")
    grad_down_e = times_first(hidden_e, upstream_column).astype(low)
    grad_down_e, d_pre_s, hidden_s = hold((grad_down_e, d_pre_s, hidden_s))
    back_down_e = scatter_far(grad_down_e, 1)
    grad_down_s = times_first(hidden_s, upstream_column).astype(low)
    grad_in_s = times_first(column, d_pre_s).astype(low)
    back_down_e, grad_down_s, grad_in_s, hidden_e, hidden_s = hold(
        (back_down_e, grad_down_s, grad_in_s, hidden_e, hidden_s)
    )
    back_down_e = scatter_near(back_down_e, 1)
    grads_s = shared_back(grad_in_s, grad_down_s, shared_shape[1])
    hidden_e, hidden_s, grads_s = hold((hidden_e, hidden_s, grads_s))
    back_s = scatter_far(grads_s, 0)
    routed_rows = (times(hidden_e, full_down) + times(hidden_s, part_down)).astype(low)
    routed_rows, back_s, inner, back_down_e = hold((routed_rows, back_s, inner, back_down_e))
    routed = column_scatter(routed_rows, 0)
    upstream = cotangent.astype(jnp.float32)
    d_mixing = mixing * (1.0 - mixing) * jnp.sum(inner[:, 1], axis=0)
    d_gates = jnp.sum(picked * inner[:, 0].T[:, None, :], axis=2)
    d_chosen = gates * (d_gates - jnp.sum(gates * d_gates, axis=1, keepdims=True))
    d_logits = jnp.sum(picked * d_chosen[:, :, None], axis=1)
    d_router_part = jnp.dot(d_logits.T, moe_wide, precision=HIGH)
    d_sigmoid_part = jnp.dot(d_mixing, moe_wide, precision=HIGH)
    d_moe = (
        d_moe
        + jnp.dot(d_logits, w_router.T, precision=HIGH)
        + d_mixing[:, None] * w_sigmoid[None, :]
    )
    d_middle_norm, d_moe_gain_part = norm_back(middle, inv_two, moe_gain, d_moe)
    d_middle = upstream + d_middle_norm
    d_middle_low, back_s, d_pre_e = hold((d_middle.astype(low), back_s, d_pre_e))
    whole_parts = gather_near(d_middle_low)
    back_s = scatter_ready(back_s, 0)
    whole_parts, back_s = hold((whole_parts, back_s))
    whole_parts = gather_far(whole_parts)
    whole_parts, back_s = hold((whole_parts, back_s))
    back_s = scatter_send(back_s, 0)
    whole_middle = gather_join(whole_parts, 0)
    d_attended = times_last(whole_middle, out_weight).astype(low)
    d_projected = attention_backward(projected, d_attended, lengths)
    small_parts = jnp.concatenate(
        [d_router_part, d_sigmoid_part[None], d_moe_gain_part[None]], axis=0
    )
    d_w_output = column_scatter(times_first(attended, whole_middle), 1)
    d_normed_rows = times_last(d_projected, in_weights).astype(low)
    d_normed_rows, d_projected, small_parts, back_s = hold(
        (d_normed_rows, d_projected, small_parts, back_s)
    )
    normed_parts = scatter_far(d_normed_rows, 0)
    d_in_weights = column_scatter(times_first(gathered_one, d_projected), 0)
    normed_parts, back_s, d_pre_e, back_down_e = hold(
        (normed_parts, back_s, d_pre_e, back_down_e)
    )
    normed_parts = scatter_near(normed_parts, 0)
    back_s = trade(scatter_sum(back_s).astype(low)[0], "dp")
    grad_gate_up = times_first(column, d_pre_e).astype(low)
    normed_parts, grad_gate_up = hold((normed_parts, grad_gate_up))
    d_expert_down = scatter_sum(back_down_e)
    back_gate_up = scatter_ready(scatter_far(grad_gate_up, 0), 0)
    d_normed = scatter_sum(normed_parts)
    d_inputs_norm, d_attn_gain_part = norm_back(inputs, inv_one, attn_gain, d_normed)
    small_sums = butterfly(
        jnp.concatenate([small_parts, d_attn_gain_part[None]], axis=0), jnp.add, ("tensor",)
    )
    back_gate_up, d_expert_down, small_sums, routed = hold(
        (back_gate_up, d_expert_down, small_sums, routed)
    )
    back_gate_up = scatter_send(back_gate_up, 0)
    d_tokens = d_middle + d_inputs_norm
    small_sums = butterfly(small_sums, jnp.add, ("dp",))
    d_attn_gain = small_sums[experts + 2]
    d_shared_gate, d_shared_up, d_shared_down = shared_back_group(back_s, *shared_shape)
    d_expert_in = scatter_sum(back_gate_up)
    clip_scale = jnp.sqrt(CLIP_LIMIT / jnp.maximum(peaks, CLIP_LIMIT))
    columns = jnp.repeat(clip_scale, DH)
    query_clipped = (w_query.astype(jnp.float32) * columns[None, :]).astype(low)
    key_clipped = (w_key.astype(jnp.float32) * columns[None, :]).astype(low)
    return (
        (middle + routed).astype(low),
        d_tokens,
        d_attn_gain,
        d_in_weights[:, :width],
        d_in_weights[:, width : 2 * width],
        d_in_weights[:, 2 * width :],
        d_w_output,
        small_sums[experts + 1],
        small_sums[:experts].T,
        small_sums[experts],
        d_shared_gate,
        d_shared_up,
        d_shared_down,
        d_expert_in[None, :, :hidden_width],
        d_expert_in[None, :, hidden_width:],
        d_expert_down[None],
        clip_scale,
        query_clipped,
        key_clipped,
    )


def solution(mesh):
    placed = (
        P(("dp", "tensor"), None),
        P("dp"),
        P(("dp", "tensor"), None),
        P(),
        P("dp", "tensor"),
        P("dp", "tensor"),
        P("dp", "tensor"),
        P("tensor", "dp"),
        P(),
        P(),
        P(),
        P("dp", "tensor"),
        P("dp", "tensor"),
        P("tensor", "dp"),
        P("dp", "tensor", None),
        P("dp", "tensor", None),
        P("dp", None, "tensor"),
        P(("dp", "tensor"), None),
    )
    return jax.shard_map(
        local,
        mesh=mesh,
        in_specs=placed,
        out_specs=(
            P(("dp", "tensor"), None),
            P(("dp", "tensor"), None),
            P(),
            P("dp", "tensor"),
            P("dp", "tensor"),
            P("dp", "tensor"),
            P("tensor", "dp"),
            P(),
            P(),
            P(),
            P("dp", "tensor"),
            P("dp", "tensor"),
            P("tensor", "dp"),
            P("dp", "tensor", None),
            P("dp", "tensor", None),
            P("dp", None, "tensor"),
            P("tensor"),
            P("dp", "tensor"),
            P("dp", "tensor"),
        ),
        check_vma=False,
    )
```
